32 devices in a mesh: rows: 8 (over y, x, core), experts: 4 (over z).
Axes of the slice: x: 2, y: 2, z: 4, core: 2. Of those that a mesh axis runs over, the one named last changes fastest.
Arguments:
- weight: bfloat16 [4, 8, 2048, 512], P('experts', None, 'rows'), may hold values from -3 to 3
- momentum: bfloat16 [4, 8, 2048, 512], P('experts', None, 'rows'), may hold values from -6 to 6
- gradient: bfloat16 [4, 8, 2048, 512], P('experts', None, 'rows'), may hold values from -32 to 32
- assign: int32 [4, 8], P('experts'), may hold values from 0 to 7, each once within a row
Outputs:
- new_weight: bfloat16 [4, 8, 2048, 512], P('experts', None, 'rows')
- new_momentum: bfloat16 [4, 8, 2048, 512], P('experts', None, 'rows')
The draws below stay inside these ranges and needn't reach their ends.
Inputs may be any that keep to these rules, and one draw needn't show every extreme that they name: Each row of assign names every slot 0 to 7 exactly once; matrix i of group e keeps its momentum in slot assign[e, i].
All inputs are finite; a program needn't handle non-finite values.
Results may differ from the reference program's by a relative error of at most 0.0075.
Values may be sent and summed in bfloat16 or wider, within the bound.
A program may use at most 64 MiB of HBM per device.

```python
import math
import jax
import jax.numpy as jnp
from jax import lax

ROWS = 2048
COLS = 512
ITERS = 5
MATS = 8
GROUPS = 4


def draw_gradient(key, part):
    fourth = jax.random.fold_in(jax.random.fold_in(key, 11), 3)
    shape = (GROUPS, MATS, ROWS, COLS)
    row_pos = jnp.arange(ROWS, dtype=jnp.float32) / max(ROWS - 1, 1)
    group_pos = jnp.arange(GROUPS, dtype=jnp.float32) / max(GROUPS - 1, 1)
    scale = (1.0 + 2.0 * row_pos)[None, None, :, None] * (1.0 + 0.75 * group_pos)[:, None, None, None]
    values = scale * jax.random.normal(fourth, shape, jnp.float32)
    return jnp.clip(values, -32.0, 32.0).astype(jnp.bfloat16)


def block_scale(stream_key, dims, cuts, low, largest):
    factor_of = 1.0
    for axis_at, shards_of in cuts:
        steps = jax.random.uniform(jax.random.fold_in(jax.random.fold_in(stream_key, 6), axis_at), (shards_of,), jnp.float32, low / len(cuts), largest / len(cuts))
        factor_of = factor_of * jnp.repeat(jnp.exp(steps), dims[axis_at] // shards_of).reshape((-1,) + (1,) * (len(dims) - 1 - axis_at))
    return factor_of


def gaussian(key, dims, scale, most, cuts=(), held_as=jnp.bfloat16):
    result = jax.random.normal(key, dims, jnp.float32) * scale
    if len(cuts) > 0:
        result = block_scale(key, dims, cuts, -0.22, 0.18) * result
    return jnp.clip(result, min=-most, max=most).astype(held_as)


def setup_inputs(seed: int = 0) -> dict:
    arg_keys = jax.random.split(jax.random.key(seed), 5)
    weight = gaussian(arg_keys[0], (GROUPS, MATS, ROWS, COLS), 0.5, 3.0, ((0, 4), (2, 8)))
    momentum = gaussian(arg_keys[1], (GROUPS, MATS, ROWS, COLS), 1.0, 6.0, ((0, 4), (2, 8)))
    gradient = draw_gradient(jax.random.fold_in(arg_keys[4], 71), 0)
    assign = jax.vmap(lambda own: jax.random.permutation(own, MATS))(jax.random.split(arg_keys[3], GROUPS)).reshape((GROUPS, MATS)).astype(jnp.int32)
    return dict(weight=weight, momentum=momentum, gradient=gradient, assign=assign)


linear_coef = 3.4445
cubic_coef = -4.775
quintic_coef = 2.0315
beta_decay = 0.95
learn_rate = 0.5
weight_decay = 0.1
norm_epsilon = 1e-07
clip_epsilon = 1e-06

def orthogonal(update):
    widened = update.astype(jnp.float32)
    iterate = (widened / (jnp.sqrt(jnp.sum(widened * widened)) + norm_epsilon)).astype(jnp.bfloat16)
    for sweep in range(ITERS):
        gram_matrix = jnp.dot(iterate.T, iterate, preferred_element_type=jnp.float32).astype(jnp.bfloat16)
        square = jnp.dot(gram_matrix, gram_matrix, preferred_element_type=jnp.float32)
        polynomial = (cubic_coef * gram_matrix.astype(jnp.float32) + quintic_coef * square).astype(jnp.bfloat16)
        iterate = (linear_coef * iterate.astype(jnp.float32) + jnp.dot(iterate, polynomial, preferred_element_type=jnp.float32)).astype(jnp.bfloat16)
    return iterate

def reference(weight, momentum, gradient, assign):
    grad_wide = gradient.astype(jnp.float32)
    sum_squares = jnp.sum(grad_wide * grad_wide)
    clip_limit = math.sqrt(float(GROUPS * MATS * ROWS * COLS))
    clip_factor = jnp.minimum(1.0, clip_limit / (jnp.sqrt(sum_squares) + clip_epsilon))
    inverse = jnp.argsort(assign, axis=1).astype(jnp.int32)
    grad_slot = jnp.take_along_axis(grad_wide, inverse[:, :, None, None], axis=1)
    state = beta_decay * momentum.astype(jnp.float32) + clip_factor * grad_slot
    update = (clip_factor * grad_slot + beta_decay * state).astype(jnp.bfloat16)
    flat = update.reshape(GROUPS * MATS, ROWS, COLS)
    ortho_slot = lax.map(orthogonal, flat).reshape(GROUPS, MATS, ROWS, COLS)
    ortho = jnp.take_along_axis(ortho_slot, assign.astype(jnp.int32)[:, :, None, None], axis=1)
    shape_scale = 0.2 * math.sqrt(max(ROWS, COLS))
    new_weight = weight.astype(jnp.float32) * (1.0 - learn_rate * weight_decay) - learn_rate * shape_scale * ortho.astype(jnp.float32)
    return (new_weight.astype(jnp.bfloat16), state.astype(jnp.bfloat16))
```

```python
import functools
import math

import jax
import jax.numpy as jnp
from jax import lax
from jax.experimental import pallas as pl
from jax.experimental.pallas import tpu as pltpu
from jax.sharding import PartitionSpec as P

ITERS = 5
linear_coef = 3.4445
cubic_coef = -4.775
quintic_coef = 2.0315
beta_decay = 0.95
learn_rate = 0.5
weight_decay = 0.1
norm_epsilon = 1e-07
clip_epsilon = 1e-06
MESH = pl.DeviceIdType.MESH
F32 = jnp.float32
BF16 = jnp.bfloat16


def gram_of(block):
    return lax.dot_general(block, block, (((0,), (0,)), ((), ())), preferred_element_type=F32)


def polynomial(gram):
    rounded = gram.astype(BF16)
    square = jnp.dot(rounded, rounded, preferred_element_type=F32)
    return (cubic_coef * rounded.astype(F32) + quintic_coef * square).astype(BF16)


def kernel(
    n, groups, block_rows,
    assign, w_hbm, m_hbm, g_hbm,
    nw_ref, nm_ref,
    w_v, m_v, g_v, out_v, mom_v, send_v, recv_v, back_v, x_v, gram_v, poly_v, row_part, group_part,
    load_sem, store_sem, rs_send, rs_recv, gs_send, gs_recv, f_send, f_recv, b_send, b_recv,
):
    me = lax.axis_index("rows")
    group = lax.axis_index("experts")
    slots, shard_rows, cols = g_v.shape

    barrier = pltpu.get_barrier_semaphore()

    def greet_row(k, carry):
        pl.semaphore_signal(barrier, inc=1, device_id={"rows": lax.rem(me + k, n)}, device_id_type=MESH)
        return carry

    def greet_group(k, carry):
        pl.semaphore_signal(
            barrier, inc=1, device_id={"experts": lax.rem(group + k, groups)}, device_id_type=MESH
        )
        return carry

    lax.fori_loop(1, n, greet_row, 0)
    lax.fori_loop(1, groups, greet_group, 0)
    load_g = pltpu.make_async_copy(g_hbm, g_v, load_sem.at[0])
    load_m = pltpu.make_async_copy(m_hbm, m_v, load_sem.at[1])
    load_w = pltpu.make_async_copy(w_hbm, w_v, load_sem.at[2])
    load_g.start()
    load_m.start()
    load_w.start()
    load_g.wait()

    def square_sum(i, total):
        wide = g_v[i].astype(F32)
        return total + jnp.sum((wide * wide).reshape(shard_rows // 8, 8, cols), axis=0)

    partial = lax.fori_loop(0, slots, square_sum, jnp.zeros((8, cols), F32))
    tile = partial[:, :128]
    for c in range(1, cols // 128):
        tile = tile + partial[:, c * 128 : (c + 1) * 128]
    row_part[me] = tile
    pl.semaphore_wait(barrier, n + groups - 2)

    def row_sum_copy(k, source):
        return pltpu.make_async_remote_copy(
            src_ref=row_part.at[me],
            dst_ref=row_part.at[source],
            send_sem=rs_send.at[k],
            recv_sem=rs_recv.at[source],
            device_id={"rows": lax.rem(me + k, n)},
            device_id_type=MESH,
        )

    def start_row(k, carry):
        row_sum_copy(k, me).start()
        return carry

    def wait_row(k, carry):
        row_sum_copy(k, lax.rem(me + k, n)).wait_recv()
        return carry

    def drain_row(k, carry):
        row_sum_copy(k, me).wait_send()
        return carry

    lax.fori_loop(1, n, start_row, 0)
    lax.fori_loop(1, n, wait_row, 0)
    group_part[group] = jnp.sum(row_part[...], axis=0)

    def group_sum_copy(k, source):
        return pltpu.make_async_remote_copy(
            src_ref=group_part.at[group],
            dst_ref=group_part.at[source],
            send_sem=gs_send.at[k],
            recv_sem=gs_recv.at[source],
            device_id={"experts": lax.rem(group + k, groups)},
            device_id_type=MESH,
        )

    def start_group(k, carry):
        group_sum_copy(k, group).start()
        return carry

    def wait_group(k, carry):
        group_sum_copy(k, lax.rem(group + k, groups)).wait_recv()
        return carry

    def drain_group(k, carry):
        group_sum_copy(k, group).wait_send()
        return carry

    lax.fori_loop(1, groups, start_group, 0)
    load_m.wait()
    lax.fori_loop(1, groups, wait_group, 0)
    sum_squares = jnp.sum(jnp.sum(group_part[...], axis=0), axis=(0, 1), keepdims=True)
    clip_limit = math.sqrt(float(slots * shard_rows * cols * n * groups))
    clip = jnp.minimum(1.0, clip_limit / (jnp.sqrt(sum_squares) + clip_epsilon))

    def forward_copy(target, source):
        return pltpu.make_async_remote_copy(
            src_ref=send_v.at[target],
            dst_ref=recv_v.at[source],
            send_sem=f_send.at[target],
            recv_sem=f_recv.at[source],
            device_id={"rows": target},
            device_id_type=MESH,
        )

    def update_of(i):
        scaled = clip * g_v[i].astype(F32)
        state = beta_decay * m_v[assign[0, i]].astype(F32) + scaled
        return (scaled + beta_decay * state).astype(BF16)

    def send_update(k, carry):
        target = lax.rem(me + k, n)
        send_v[target] = update_of(target)
        forward_copy(target, me).start()
        return carry

    lax.fori_loop(1, n, send_update, 0)
    own = update_of(me)
    recv_v[me] = own
    gram_v[...] = gram_of(own)

    def momentum_of(p, carry):
        index = lax.fori_loop(
            0, slots, lambda i, found: jnp.where(assign[0, i] == p, i, found), jnp.int32(0)
        )
        mom_v[p] = (
            beta_decay * m_v[p].astype(F32) + clip * g_v[index].astype(F32)
        ).astype(BF16)
        return carry

    lax.fori_loop(0, slots, momentum_of, 0)
    store_m = pltpu.make_async_copy(mom_v, nm_ref, store_sem.at[0])
    store_m.start()

    def take_update(k, carry):
        source = lax.rem(me + k, n)
        forward_copy(source, source).wait_recv()
        gram_v[...] += gram_of(recv_v[source])
        return carry

    lax.fori_loop(1, n, take_update, 0)

    gram = gram_v[...]
    diagonal = lax.broadcasted_iota(jnp.int32, gram.shape, 0) == lax.broadcasted_iota(
        jnp.int32, gram.shape, 1
    )
    trace = jnp.sum(jnp.where(diagonal, gram, 0.0), axis=(0, 1), keepdims=True)
    scale = 1.0 / (jnp.sqrt(trace) + norm_epsilon)
    poly_v[...] = polynomial(gram * scale * scale)

    shards = block_rows // shard_rows
    for b in range(n // shards):
        x = recv_v[pl.ds(b * shards, shards)].reshape(block_rows, cols)
        product = jnp.dot(x, poly_v[...], preferred_element_type=F32)
        x = (scale * (linear_coef * x.astype(F32) + product)).astype(BF16)
        x_v[pl.ds(b * block_rows, block_rows)] = x
        if b == 0:
            gram_v[...] = gram_of(x)
        else:
            gram_v[...] += gram_of(x)

    def sweep(t, carry):
        poly_v[...] = polynomial(gram_v[...])
        for b in range(n // shards):
            rows = pl.ds(b * block_rows, block_rows)
            x = x_v[rows]
            product = jnp.dot(x, poly_v[...], preferred_element_type=F32)
            x = (linear_coef * x.astype(F32) + product).astype(BF16)
            x_v[rows] = x
            if b == 0:
                gram_v[...] = gram_of(x)
            else:
                gram_v[...] += gram_of(x)
        return carry

    lax.fori_loop(1, ITERS - 1, sweep, 0)
    poly_v[...] = polynomial(gram_v[...])

    def last_rows(i):
        x = x_v[pl.ds(pl.multiple_of(i * shard_rows, shard_rows), shard_rows)]
        product = jnp.dot(x, poly_v[...], preferred_element_type=F32)
        return (linear_coef * x.astype(F32) + product).astype(BF16)

    def back_copy(target, source):
        return pltpu.make_async_remote_copy(
            src_ref=send_v.at[target],
            dst_ref=back_v.at[source],
            send_sem=b_send.at[target],
            recv_sem=b_recv.at[source],
            device_id={"rows": target},
            device_id_type=MESH,
        )

    def send_back(k, carry):
        target = lax.rem(me + k, n)
        forward_copy(target, me).wait_send()
        send_v[target] = last_rows(target)
        back_copy(target, me).start()
        return carry

    lax.fori_loop(1, n, send_back, 0)
    step = learn_rate * 0.2 * math.sqrt(max(n * shard_rows, cols))
    load_w.wait()

    def weight_of(i, ortho):
        out_v[i] = (
            w_v[i].astype(F32) * (1.0 - learn_rate * weight_decay) - step * ortho.astype(F32)
        ).astype(BF16)
        pltpu.make_async_copy(out_v.at[i], nw_ref.at[i], f_send.at[i]).start()

    weight_of(me, last_rows(me))

    def take_back(k, carry):
        source = lax.rem(me + k, n)
        back_copy(source, source).wait_recv()
        weight_of(source, back_v[source])
        return carry

    lax.fori_loop(1, n, take_back, 0)
    lax.fori_loop(1, n, drain_row, 0)
    lax.fori_loop(1, groups, drain_group, 0)

    def drain_back(k, carry):
        back_copy(lax.rem(me + k, n), me).wait_send()
        return carry

    lax.fori_loop(1, n, drain_back, 0)

    def drain_out(i, carry):
        pltpu.make_async_copy(out_v.at[i], nw_ref.at[i], f_send.at[i]).wait()
        return carry

    lax.fori_loop(0, n, drain_out, 0)
    store_m.wait()


def local(weight, momentum, gradient, assign):
    n = lax.axis_size("rows")
    groups = lax.axis_size("experts")
    _, slots, shard_rows, cols = gradient.shape
    assert slots == n
    block_rows = min(1024, n * shard_rows)
    shape = (slots, shard_rows, cols)
    new_weight, new_momentum = pl.pallas_call(
        functools.partial(kernel, n, groups, block_rows),
        out_shape=(jax.ShapeDtypeStruct(shape, BF16),) * 2,
        in_specs=[pl.BlockSpec(memory_space=pltpu.SMEM)] + [pl.BlockSpec(memory_space=pl.ANY)] * 3,
        out_specs=(pl.BlockSpec(memory_space=pl.ANY),) * 2,
        scratch_shapes=[pltpu.VMEM(shape, BF16)] * 8
        + [
            pltpu.VMEM((n * shard_rows, cols), BF16),
            pltpu.VMEM((cols, cols), F32),
            pltpu.VMEM((cols, cols), BF16),
            pltpu.VMEM((n, 8, 128), F32),
            pltpu.VMEM((groups, 8, 128), F32),
            pltpu.SemaphoreType.DMA((3,)),
            pltpu.SemaphoreType.DMA((1,)),
            pltpu.SemaphoreType.DMA((n,)),
            pltpu.SemaphoreType.DMA((n,)),
            pltpu.SemaphoreType.DMA((groups,)),
            pltpu.SemaphoreType.DMA((groups,)),
            pltpu.SemaphoreType.DMA((n,)),
            pltpu.SemaphoreType.DMA((n,)),
            pltpu.SemaphoreType.DMA((n,)),
            pltpu.SemaphoreType.DMA((n,)),
        ],
        compiler_params=pltpu.CompilerParams(
            collective_id=0, has_side_effects=True, vmem_limit_bytes=48 << 20
        ),
        name="muon_step",
    )(assign, weight[0], momentum[0], gradient[0])
    return new_weight[None], new_momentum[None]


def solution(mesh):
    placed = P("experts", None, "rows", None)
    return jax.shard_map(
        local,
        mesh=mesh,
        in_specs=(placed, placed, placed, P("experts", None)),
        out_specs=(placed, placed),
        check_vma=False,
    )
```

```python
import functools
import math

import jax
import jax.numpy as jnp
from jax import lax
from jax.experimental import pallas as pl
from jax.experimental.pallas import tpu as pltpu
from jax.sharding import PartitionSpec as P

ITERS = 5
first_steps = 3
linear_coef = 3.4445
cubic_coef = -4.775
quintic_coef = 2.0315
beta_decay = 0.95
learn_rate = 0.5
weight_decay = 0.1
norm_epsilon = 1e-07
clip_epsilon = 1e-06
MESH = pl.DeviceIdType.MESH
F32 = jnp.float32
BF16 = jnp.bfloat16


def gram_of(block):
    return lax.dot_general(block, block, (((0,), (0,)), ((), ())), preferred_element_type=F32)


def dot(a, b):
    return jnp.dot(a, b, preferred_element_type=F32)


def factor(gram):
    rows = lax.broadcasted_iota(jnp.int32, gram.shape, 0)
    columns = lax.broadcasted_iota(jnp.int32, gram.shape, 1)
    wide = cubic_coef * gram.astype(F32) + quintic_coef * dot(gram, gram)
    return jnp.where(rows == columns, wide + linear_coef, wide).astype(BF16)


def chain(steps, split, gram_v, poly_v):
    for t in range(steps):
        gram = gram_v[...]
        high = gram.astype(BF16)
        q = factor(high)
        if t < steps - 1:
            half = dot(high, q)
            if split:
                half += dot((gram - high.astype(F32)).astype(BF16), q)
            gram_v[...] = dot(half.astype(BF16), q)
        poly_v[...] = q if t == 0 else dot(poly_v[...], q).astype(BF16)


def kernel(
    n, groups, block_rows,
    assign, w_hbm, m_hbm, g_hbm,
    nw_ref, nm_ref,
    w_v, m_v, g_v, send_v, recv_v, back_v, x_v, gram_v, poly_v, part,
    load_sem, s_send, s_recv, f_send, f_recv, b_send, b_recv,
):
    me = lax.axis_index("rows")
    group = lax.axis_index("experts")
    slots, shard_rows, cols = g_v.shape

    barrier = pltpu.get_barrier_semaphore()

    devices = n * groups
    here = group * n + me

    def device(k):
        index = lax.rem(here + k, devices)
        return index, {"experts": index // n, "rows": lax.rem(index, n)}

    def greet(k, carry):
        pl.semaphore_signal(barrier, inc=1, device_id=device(k)[1], device_id_type=MESH)
        return carry

    lax.fori_loop(1, devices, greet, 0)
    load_g = pltpu.make_async_copy(g_hbm, g_v, load_sem.at[0])
    load_m = pltpu.make_async_copy(m_hbm, m_v, load_sem.at[1])
    load_w = pltpu.make_async_copy(w_hbm, w_v, load_sem.at[2])
    load_g.start()
    load_m.start()
    load_w.start()
    load_g.wait()

    def square_sum(i, total):
        wide = g_v[i].astype(F32)
        return total + jnp.sum((wide * wide).reshape(shard_rows // 8, 8, cols), axis=0)

    partial = lax.fori_loop(0, slots, square_sum, jnp.zeros((8, cols), F32))
    tile = partial[:, :128]
    for c in range(1, cols // 128):
        tile = tile + partial[:, c * 128 : (c + 1) * 128]
    part[here] = tile
    pl.semaphore_wait(barrier, devices - 1)

    def sum_copy(k, source):
        return pltpu.make_async_remote_copy(
            src_ref=part.at[here],
            dst_ref=part.at[source],
            send_sem=s_send.at[k],
            recv_sem=s_recv.at[source],
            device_id=device(k)[1],
            device_id_type=MESH,
        )

    def start_sum(k, carry):
        sum_copy(k, here).start()
        return carry

    def wait_sum(k, carry):
        sum_copy(k, device(k)[0]).wait_recv()
        return carry

    def drain_sum(k, carry):
        sum_copy(k, here).wait_send()
        return carry

    lax.fori_loop(1, devices, start_sum, 0)
    load_m.wait()
    lax.fori_loop(1, devices, wait_sum, 0)
    sum_squares = jnp.sum(jnp.sum(part[...], axis=0), axis=(0, 1), keepdims=True)
    clip_limit = math.sqrt(float(slots * shard_rows * cols * n * groups))
    clip = jnp.minimum(1.0, clip_limit / (jnp.sqrt(sum_squares) + clip_epsilon))

    def forward_copy(target, source):
        return pltpu.make_async_remote_copy(
            src_ref=send_v.at[target],
            dst_ref=recv_v.at[source],
            send_sem=f_send.at[target],
            recv_sem=f_recv.at[source],
            device_id={"rows": target},
            device_id_type=MESH,
        )

    def update_of(i):
        scaled = clip * g_v[i].astype(F32)
        state = beta_decay * m_v[assign[0, i]].astype(F32) + scaled
        return (scaled + beta_decay * state).astype(BF16)

    def peer(k):
        return lax.rem(me + 1 + lax.rem(k, n - 1), n)

    def send_update(k, carry):
        target = peer(k)
        send_v[target] = update_of(target)
        forward_copy(target, me).start()
        return carry

    lax.fori_loop(1, n, send_update, 0)
    own = update_of(me)
    recv_v[me] = own
    gram_v[...] = gram_of(own)

    def momentum_of(p, carry):
        index = lax.fori_loop(
            0, slots, lambda i, found: jnp.where(assign[0, i] == p, i, found), jnp.int32(0)
        )
        nm_ref[p] = (
            beta_decay * m_v[p].astype(F32) + clip * g_v[index].astype(F32)
        ).astype(BF16)
        return carry

    lax.fori_loop(0, slots, momentum_of, 0)

    def take_update(k, carry):
        source = lax.rem(me + n - 1 - lax.rem(k, n - 1), n)
        forward_copy(source, source).wait_recv()
        gram_v[...] += gram_of(recv_v[source])
        return carry

    lax.fori_loop(1, n, take_update, 0)

    gram = gram_v[...]
    diagonal = lax.broadcasted_iota(jnp.int32, gram.shape, 0) == lax.broadcasted_iota(
        jnp.int32, gram.shape, 1
    )
    trace = jnp.sum(jnp.where(diagonal, gram, 0.0), axis=(0, 1), keepdims=True)
    scale = 1.0 / (jnp.sqrt(trace) + norm_epsilon)
    gram_v[...] = gram * (scale * scale)
    chain(first_steps, True, gram_v, poly_v)

    shards = block_rows // shard_rows
    for b in range(n // shards):
        x = recv_v[pl.ds(b * shards, shards)].reshape(block_rows, cols)
        x = (scale * dot(x, poly_v[...])).astype(BF16)
        x_v[pl.ds(b * block_rows, block_rows)] = x
        if b == 0:
            gram_v[...] = gram_of(x)
        else:
            gram_v[...] += gram_of(x)

    chain(ITERS - first_steps, False, gram_v, poly_v)

    def last_rows(i):
        x = x_v[pl.ds(pl.multiple_of(i * shard_rows, shard_rows), shard_rows)]
        return dot(x, poly_v[...]).astype(BF16)

    def back_copy(target, source):
        return pltpu.make_async_remote_copy(
            src_ref=send_v.at[target],
            dst_ref=back_v.at[source],
            send_sem=b_send.at[target],
            recv_sem=b_recv.at[source],
            device_id={"rows": target},
            device_id_type=MESH,
        )

    def send_back(k, carry):
        target = peer(k)
        forward_copy(target, me).wait_send()
        send_v[target] = last_rows(target)
        back_copy(target, me).start()
        return carry

    lax.fori_loop(1, n, send_back, 0)
    step = learn_rate * 0.2 * math.sqrt(max(n * shard_rows, cols))
    load_w.wait()

    def weight_of(i, ortho):
        nw_ref[i] = (
            w_v[i].astype(F32) * (1.0 - learn_rate * weight_decay) - step * ortho.astype(F32)
        ).astype(BF16)

    weight_of(me, last_rows(me))

    def take_back(k, carry):
        source = lax.rem(me + n - 1 - lax.rem(k, n - 1), n)
        back_copy(source, source).wait_recv()
        weight_of(source, back_v[source])
        return carry

    lax.fori_loop(1, n, take_back, 0)
    lax.fori_loop(1, devices, drain_sum, 0)

    def drain_back(k, carry):
        back_copy(lax.rem(me + k, n), me).wait_send()
        return carry

    lax.fori_loop(1, n, drain_back, 0)


def local(weight, momentum, gradient, assign):
    n = lax.axis_size("rows")
    groups = lax.axis_size("experts")
    _, slots, shard_rows, cols = gradient.shape
    assert slots == n
    block_rows = min(1024, n * shard_rows)
    shape = (slots, shard_rows, cols)
    new_weight, new_momentum = pl.pallas_call(
        functools.partial(kernel, n, groups, block_rows),
        out_shape=(jax.ShapeDtypeStruct(shape, BF16),) * 2,
        in_specs=[pl.BlockSpec(memory_space=pltpu.SMEM)] + [pl.BlockSpec(memory_space=pl.ANY)] * 3,
        out_specs=(pl.BlockSpec(memory_space=pltpu.VMEM),) * 2,
        scratch_shapes=[pltpu.VMEM(shape, BF16)] * 6
        + [
            pltpu.VMEM((n * shard_rows, cols), BF16),
            pltpu.VMEM((cols, cols), F32),
            pltpu.VMEM((cols, cols), BF16),
            pltpu.VMEM((n * groups, 8, 128), F32),
            pltpu.SemaphoreType.DMA((3,)),
            pltpu.SemaphoreType.DMA((n * groups,)),
            pltpu.SemaphoreType.DMA((n * groups,)),
            pltpu.SemaphoreType.DMA((n,)),
            pltpu.SemaphoreType.DMA((n,)),
            pltpu.SemaphoreType.DMA((n,)),
            pltpu.SemaphoreType.DMA((n,)),
        ],
        compiler_params=pltpu.CompilerParams(
            collective_id=0, has_side_effects=True, vmem_limit_bytes=48 << 20
        ),
        name="muon_step",
    )(assign, weight[0], momentum[0], gradient[0])
    return new_weight[None], new_momentum[None]


def solution(mesh):
    placed = P("experts", None, "rows", None)
    return jax.shard_map(
        local,
        mesh=mesh,
        in_specs=(placed, placed, placed, P("experts", None)),
        out_specs=(placed, placed),
        check_vma=False,
    )
```

```python
import functools
import math

import jax
import jax.numpy as jnp
from jax import lax
from jax.experimental import pallas as pl
from jax.experimental.pallas import tpu as pltpu
from jax.sharding import PartitionSpec as P

ITERS = 5
first_steps = 3
linear_coef = 3.4445
cubic_coef = -4.775
quintic_coef = 2.0315
beta_decay = 0.95
learn_rate = 0.5
weight_decay = 0.1
norm_epsilon = 1e-07
clip_epsilon = 1e-06
MESH = pl.DeviceIdType.MESH
F32 = jnp.float32
BF16 = jnp.bfloat16


def gram_of(block):
    return lax.dot_general(block, block, (((0,), (0,)), ((), ())), preferred_element_type=F32)


def dot(a, b):
    return jnp.dot(a, b, preferred_element_type=F32)


def factor(gram):
    rows = lax.broadcasted_iota(jnp.int32, gram.shape, 0)
    columns = lax.broadcasted_iota(jnp.int32, gram.shape, 1)
    wide = cubic_coef * gram.astype(F32) + quintic_coef * dot(gram, gram)
    return jnp.where(rows == columns, wide + linear_coef, wide).astype(BF16)


def chain(steps, split, gram_v, poly_v):
    for t in range(steps):
        gram = gram_v[...]
        high = gram.astype(BF16)
        q = factor(high)
        if t < steps - 1:
            half = dot(high, q)
            if split:
                half += dot((gram - high.astype(F32)).astype(BF16), q)
            gram_v[...] = dot(half.astype(BF16), q)
        poly_v[...] = q if t == 0 else dot(poly_v[...], q).astype(BF16)


def kernel(
    n, groups, block_rows,
    assign, w_hbm, m_hbm, g_hbm,
    nw_ref, nm_ref,
    w_v, m_v, g_v, send_v, recv_v, gram_v, poly_v, first_v, part, pack,
    load_sem, s_send, s_recv, f_send, f_recv, p_send, p_recv,
):
    me = lax.axis_index("rows")
    group = lax.axis_index("experts")
    slots, shard_rows, cols = g_v.shape

    barrier = pltpu.get_barrier_semaphore()

    devices = n * groups
    here = group * n + me

    def device(k):
        index = lax.rem(here + k, devices)
        return index, {"experts": index // n, "rows": lax.rem(index, n)}

    def greet(k, carry):
        pl.semaphore_signal(barrier, inc=1, device_id=device(k)[1], device_id_type=MESH)
        return carry

    lax.fori_loop(1, devices, greet, 0)
    load_g = pltpu.make_async_copy(g_hbm, g_v, load_sem.at[0])
    load_m = pltpu.make_async_copy(m_hbm, m_v, load_sem.at[1])
    load_w = pltpu.make_async_copy(w_hbm, w_v, load_sem.at[2])
    load_g.start()
    load_m.start()
    load_w.start()
    load_g.wait()

    def square_sum(i, total):
        wide = g_v[i].astype(F32)
        return total + jnp.sum((wide * wide).reshape(shard_rows // 8, 8, cols), axis=0)

    partial = lax.fori_loop(0, slots, square_sum, jnp.zeros((8, cols), F32))
    tile = partial[:, :128]
    for c in range(1, cols // 128):
        tile = tile + partial[:, c * 128 : (c + 1) * 128]
    part[here] = tile
    pl.semaphore_wait(barrier, devices - 1)

    def sum_copy(k, source):
        return pltpu.make_async_remote_copy(
            src_ref=part.at[here],
            dst_ref=part.at[source],
            send_sem=s_send.at[k],
            recv_sem=s_recv.at[source],
            device_id=device(k)[1],
            device_id_type=MESH,
        )

    def start_sum(k, carry):
        sum_copy(k, here).start()
        return carry

    def wait_sum(k, carry):
        sum_copy(k, device(k)[0]).wait_recv()
        return carry

    def drain_sum(k, carry):
        sum_copy(k, here).wait_send()
        return carry

    lax.fori_loop(1, devices, start_sum, 0)
    load_m.wait()
    lax.fori_loop(1, devices, wait_sum, 0)
    sum_squares = jnp.sum(jnp.sum(part[...], axis=0), axis=(0, 1), keepdims=True)
    clip_limit = math.sqrt(float(slots * shard_rows * cols * n * groups))
    clip = jnp.minimum(1.0, clip_limit / (jnp.sqrt(sum_squares) + clip_epsilon))

    def forward_copy(target, source):
        return pltpu.make_async_remote_copy(
            src_ref=send_v.at[target],
            dst_ref=recv_v.at[source],
            send_sem=f_send.at[target],
            recv_sem=f_recv.at[source],
            device_id={"rows": target},
            device_id_type=MESH,
        )

    def update_of(i):
        scaled = clip * g_v[i].astype(F32)
        state = beta_decay * m_v[assign[0, i]].astype(F32) + scaled
        return (scaled + beta_decay * state).astype(BF16)

    def peer(k):
        return lax.rem(me + 1 + lax.rem(k, n - 1), n)

    def send_update(k, carry):
        target = peer(k)
        send_v[target] = update_of(target)
        forward_copy(target, me).start()
        return carry

    lax.fori_loop(1, n, send_update, 0)
    own = update_of(me)
    recv_v[me] = own
    send_v[me] = own
    gram_v[...] = gram_of(own)

    def momentum_of(p, carry):
        index = lax.fori_loop(
            0, slots, lambda i, found: jnp.where(assign[0, i] == p, i, found), jnp.int32(0)
        )
        nm_ref[p] = (
            beta_decay * m_v[p].astype(F32) + clip * g_v[index].astype(F32)
        ).astype(BF16)
        return carry

    lax.fori_loop(0, slots, momentum_of, 0)

    def take_update(k, carry):
        source = lax.rem(me + n - 1 - lax.rem(k, n - 1), n)
        forward_copy(source, source).wait_recv()
        gram_v[...] += gram_of(recv_v[source])
        return carry

    lax.fori_loop(1, n, take_update, 0)

    gram = gram_v[...]
    diagonal = lax.broadcasted_iota(jnp.int32, gram.shape, 0) == lax.broadcasted_iota(
        jnp.int32, gram.shape, 1
    )
    trace = jnp.sum(jnp.where(diagonal, gram, 0.0), axis=(0, 1), keepdims=True)
    scale = 1.0 / (jnp.sqrt(trace) + norm_epsilon)
    gram_v[...] = gram * (scale * scale)
    chain(first_steps, True, gram_v, first_v)

    shards = block_rows // shard_rows
    for b in range(n // shards):
        x = recv_v[pl.ds(b * shards, shards)].reshape(block_rows, cols)
        x = (scale * dot(x, first_v[...])).astype(BF16)
        if b == 0:
            gram_v[...] = gram_of(x)
        else:
            gram_v[...] += gram_of(x)

    chain(ITERS - first_steps, False, gram_v, poly_v)

    whole = (scale * dot(first_v[...], poly_v[...])).astype(BF16)
    half = cols // 2
    piece = half // 2
    for q in range(2):
        top = slice(q * piece, (q + 1) * piece)
        bottom = slice(half + q * piece, half + (q + 1) * piece)
        pack[me, q, 0] = whole[top, :half]
        pack[me, q, 1] = whole[top, half:]
        pack[me, q, 2] = whole[bottom, half:]

    bits = (n // 2).bit_length() - 1
    orders = (tuple(range(bits)), tuple(reversed(range(bits))))

    def flip(index, bit):
        return index + bit * (1 - 2 * lax.rem(lax.div(index, bit), 2))

    def owner_of(mask):
        index = me
        for b in range(bits):
            if mask >> b & 1:
                index = flip(index, 2 << b)
        return index

    def onward(mask, q):
        last = max((orders[q].index(b) for b in range(bits) if mask >> b & 1), default=-1)
        return orders[q][last + 1 :]

    sent = []

    def send_piece(owner, q, target):
        copy = pltpu.make_async_remote_copy(
            src_ref=pack.at[owner, q],
            dst_ref=pack.at[owner, q],
            send_sem=p_send.at[len(sent)],
            recv_sem=p_recv.at[owner, q],
            device_id={"rows": target},
            device_id_type=MESH,
        )
        copy.start()
        sent.append(copy)

    def wait_piece(owner, q):
        pltpu.make_async_remote_copy(
            src_ref=pack.at[owner, q],
            dst_ref=pack.at[owner, q],
            send_sem=p_send.at[0],
            recv_sem=p_recv.at[owner, q],
            device_id={"rows": flip(me, 1)},
            device_id_type=MESH,
        ).wait_recv()

    step = learn_rate * 0.2 * math.sqrt(max(n * shard_rows, cols))

    def weight_of(i):
        left = send_v[i, :, :half]
        right = send_v[i, :, half:]
        first, cross, second = (
            jnp.concatenate([pack[i, 0, b], pack[i, 1, b]], axis=0) for b in range(3)
        )
        mirrored = lax.dot_general(right, cross, (((1,), (1,)), ((), ())), preferred_element_type=F32)
        decay = 1.0 - learn_rate * weight_decay
        nw_ref[i, :, :half] = (
            w_v[i, :, :half].astype(F32) * decay - step * (dot(left, first) + mirrored)
        ).astype(BF16)
        nw_ref[i, :, half:] = (
            w_v[i, :, half:].astype(F32) * decay - step * (dot(left, cross) + dot(right, second))
        ).astype(BF16)

    for level in range(bits):
        for q in range(2):
            send_piece(me, q, flip(me, 2 << orders[q][level]))
    for q in range(2):
        send_piece(me, q, flip(me, 1))
    load_w.wait()
    weight_of(me)
    masks = [[m for m in range(n // 2) if bin(m).count("1") == level] for level in range(bits + 1)]
    for level in range(bits + 1):
        if level > 0:
            pieces = [(m, q) for m in masks[level] for q in range(2)]
            for m, q in sorted(pieces, key=lambda at: -len(onward(*at))):
                wait_piece(owner_of(m), q)
                for b in onward(m, q):
                    send_piece(owner_of(m), q, flip(me, 2 << b))
                send_piece(owner_of(m), q, flip(me, 1))
            for m in masks[level]:
                weight_of(owner_of(m))
        for m in masks[level]:
            owner = flip(owner_of(m), 1)
            for q in range(2):
                wait_piece(owner, q)
            weight_of(owner)

    def drain_forward(k, carry):
        forward_copy(peer(k), me).wait_send()
        return carry

    lax.fori_loop(1, n, drain_forward, 0)
    lax.fori_loop(1, devices, drain_sum, 0)
    for copy in sent:
        copy.wait_send()


def local(weight, momentum, gradient, assign):
    n = lax.axis_size("rows")
    groups = lax.axis_size("experts")
    _, slots, shard_rows, cols = gradient.shape
    assert slots == n and n & (n - 1) == 0
    block_rows = min(1024, n * shard_rows)
    shape = (slots, shard_rows, cols)
    new_weight, new_momentum = pl.pallas_call(
        functools.partial(kernel, n, groups, block_rows),
        out_shape=(jax.ShapeDtypeStruct(shape, BF16),) * 2,
        in_specs=[pl.BlockSpec(memory_space=pltpu.SMEM)] + [pl.BlockSpec(memory_space=pl.ANY)] * 3,
        out_specs=(pl.BlockSpec(memory_space=pltpu.VMEM),) * 2,
        scratch_shapes=[pltpu.VMEM(shape, BF16)] * 5
        + [
            pltpu.VMEM((cols, cols), F32),
            pltpu.VMEM((cols, cols), BF16),
            pltpu.VMEM((cols, cols), BF16),
            pltpu.VMEM((n * groups, 8, 128), F32),
            pltpu.VMEM((n, 2, 3, cols // 4, cols // 2), BF16),
            pltpu.SemaphoreType.DMA((3,)),
            pltpu.SemaphoreType.DMA((n * groups,)),
            pltpu.SemaphoreType.DMA((n * groups,)),
            pltpu.SemaphoreType.DMA((n,)),
            pltpu.SemaphoreType.DMA((n,)),
            pltpu.SemaphoreType.DMA((2 * n,)),
            pltpu.SemaphoreType.DMA((n, 2)),
        ],
        compiler_params=pltpu.CompilerParams(
            collective_id=0, has_side_effects=True, vmem_limit_bytes=48 << 20
        ),
        name="muon_step",
    )(assign, weight[0], momentum[0], gradient[0])
    return new_weight[None], new_momentum[None]


def solution(mesh):
    placed = P("experts", None, "rows", None)
    return jax.shard_map(
        local,
        mesh=mesh,
        in_specs=(placed, placed, placed, P("experts", None)),
        out_specs=(placed, placed),
        check_vma=False,
    )
```

```python
import functools
import math

import jax
import jax.numpy as jnp
from jax import lax
from jax.experimental import pallas as pl
from jax.experimental.pallas import tpu as pltpu
from jax.sharding import PartitionSpec as P

ITERS = 5
first_steps = 3
tiles = 4
linear_coef = 3.4445
cubic_coef = -4.775
quintic_coef = 2.0315
beta_decay = 0.95
learn_rate = 0.5
weight_decay = 0.1
norm_epsilon = 1e-07
clip_epsilon = 1e-06
MESH = pl.DeviceIdType.MESH
F32 = jnp.float32
BF16 = jnp.bfloat16


def gram_of(block):
    return lax.dot_general(block, block, (((0,), (0,)), ((), ())), preferred_element_type=F32)


def dot(a, b):
    return jnp.dot(a, b, preferred_element_type=F32)


def factor(gram):
    rows = lax.broadcasted_iota(jnp.int32, gram.shape, 0)
    columns = lax.broadcasted_iota(jnp.int32, gram.shape, 1)
    wide = cubic_coef * gram.astype(F32) + quintic_coef * dot(gram, gram)
    return jnp.where(rows == columns, wide + linear_coef, wide).astype(BF16)


def chain(steps, split, gram_v, poly_v):
    for t in range(steps):
        gram = gram_v[...]
        high = gram.astype(BF16)
        q = factor(high)
        if t < steps - 1:
            half = dot(high, q)
            if split:
                half += dot((gram - high.astype(F32)).astype(BF16), q)
            gram_v[...] = dot(half.astype(BF16), q)
        poly_v[...] = q if t == 0 else dot(poly_v[...], q).astype(BF16)


def kernel(
    n, groups, block_rows,
    assign_hbm, w_hbm, m_hbm, g_hbm,
    nw_ref, nm_ref,
    w_v, m_v, g_v, send_v, recv_v, gram_v, poly_v, first_v, part, pack, full_v, assign,
    load_sem, g_sem, s_send, s_recv, f_send, f_recv, p_send, p_recv,
):
    me = lax.axis_index("rows")
    group = lax.axis_index("experts")
    slots, shard_rows, cols = g_v.shape

    barrier = pltpu.get_barrier_semaphore()

    devices = n * groups
    here = group * n + me

    def device(k):
        index = lax.rem(here + k, devices)
        return index, {"experts": index // n, "rows": lax.rem(index, n)}

    def greet(k, carry):
        pl.semaphore_signal(barrier, inc=1, device_id=device(k)[1], device_id_type=MESH)
        return carry

    lax.fori_loop(1, devices, greet, 0)

    def load_g(i):
        return pltpu.make_async_copy(g_hbm.at[i], g_v.at[i], g_sem.at[i])

    def start_g(i, carry):
        load_g(i).start()
        return carry

    lax.fori_loop(0, slots, start_g, 0)
    load_a = pltpu.make_async_copy(assign_hbm, assign, load_sem.at[0])
    load_m = pltpu.make_async_copy(m_hbm, m_v, load_sem.at[1])
    load_w = pltpu.make_async_copy(w_hbm, w_v, load_sem.at[2])
    load_a.start()
    load_m.start()
    load_w.start()

    def square_sum(i, total):
        load_g(i).wait()
        wide = g_v[i].astype(F32)
        return total + jnp.sum((wide * wide).reshape(shard_rows // 8, 8, cols), axis=0)

    partial = lax.fori_loop(0, slots, square_sum, jnp.zeros((8, cols), F32))
    tile = partial[:, :128]
    for c in range(1, cols // 128):
        tile = tile + partial[:, c * 128 : (c + 1) * 128]
    part[here] = tile
    pl.semaphore_wait(barrier, devices - 1)

    def sum_copy(k, source):
        return pltpu.make_async_remote_copy(
            src_ref=part.at[here],
            dst_ref=part.at[source],
            send_sem=s_send.at[k],
            recv_sem=s_recv.at[source],
            device_id=device(k)[1],
            device_id_type=MESH,
        )

    def start_sum(k, carry):
        sum_copy(k, here).start()
        return carry

    def wait_sum(k, carry):
        sum_copy(k, device(k)[0]).wait_recv()
        return carry

    def drain_sum(k, carry):
        sum_copy(k, here).wait_send()
        return carry

    lax.fori_loop(1, devices, start_sum, 0)
    load_m.wait()
    load_a.wait()
    lax.fori_loop(1, devices, wait_sum, 0)
    sum_squares = jnp.sum(jnp.sum(part[...], axis=0), axis=(0, 1), keepdims=True)
    clip_limit = math.sqrt(float(slots * shard_rows * cols * n * groups))
    clip = jnp.minimum(1.0, clip_limit / (jnp.sqrt(sum_squares) + clip_epsilon))

    def forward_copy(target, source):
        return pltpu.make_async_remote_copy(
            src_ref=send_v.at[target],
            dst_ref=recv_v.at[source],
            send_sem=f_send.at[target],
            recv_sem=f_recv.at[source],
            device_id={"rows": target},
            device_id_type=MESH,
        )

    def update_of(i):
        scaled = clip * g_v[i].astype(F32)
        state = beta_decay * m_v[assign[0, i]].astype(F32) + scaled
        return (scaled + beta_decay * state).astype(BF16)

    def peer(k):
        return lax.rem(me + 1 + lax.rem(k, n - 1), n)

    def send_update(k, carry):
        target = peer(k)
        send_v[target] = update_of(target)
        forward_copy(target, me).start()
        return carry

    lax.fori_loop(1, n, send_update, 0)
    own = update_of(me)
    recv_v[me] = own
    send_v[me] = own
    gram_v[...] = gram_of(own)

    def momentum_of(p, carry):
        index = lax.fori_loop(
            0, slots, lambda i, found: jnp.where(assign[0, i] == p, i, found), jnp.int32(0)
        )
        nm_ref[p] = (
            beta_decay * m_v[p].astype(F32) + clip * g_v[index].astype(F32)
        ).astype(BF16)
        return carry

    lax.fori_loop(0, slots, momentum_of, 0)

    def take_update(k, carry):
        source = lax.rem(me + n - 1 - lax.rem(k, n - 1), n)
        forward_copy(source, source).wait_recv()
        gram_v[...] += gram_of(recv_v[source])
        return carry

    lax.fori_loop(1, n, take_update, 0)

    gram = gram_v[...]
    diagonal = lax.broadcasted_iota(jnp.int32, gram.shape, 0) == lax.broadcasted_iota(
        jnp.int32, gram.shape, 1
    )
    trace = jnp.sum(jnp.where(diagonal, gram, 0.0), axis=(0, 1), keepdims=True)
    scale = 1.0 / (jnp.sqrt(trace) + norm_epsilon)
    gram_v[...] = gram * (scale * scale)
    chain(first_steps, True, gram_v, first_v)

    shards = block_rows // shard_rows
    for b in range(n // shards):
        x = recv_v[pl.ds(b * shards, shards)].reshape(block_rows, cols)
        x = (scale * dot(x, first_v[...])).astype(BF16)
        if b == 0:
            gram_v[...] = gram_of(x)
        else:
            gram_v[...] += gram_of(x)

    chain(ITERS - first_steps, False, gram_v, poly_v)

    whole = (scale * dot(first_v[...], poly_v[...])).astype(BF16)
    side = cols // tiles
    places = [(r, c) for r in range(tiles) for c in range(r, tiles)]
    half = len(places) // 2

    def cut(r):
        return slice(r * side, (r + 1) * side)

    for at, (r, c) in enumerate(places):
        pack[me, at // half, at % half] = whole[cut(r), cut(c)]

    bits = (n // 2).bit_length() - 1
    orders = (tuple(range(bits)), tuple(reversed(range(bits))))

    def flip(index, bit):
        return index + bit * (1 - 2 * lax.rem(lax.div(index, bit), 2))

    def owner_of(mask):
        index = me
        for b in range(bits):
            if mask >> b & 1:
                index = flip(index, 2 << b)
        return index

    def onward(mask, q):
        last = max((orders[q].index(b) for b in range(bits) if mask >> b & 1), default=-1)
        return orders[q][last + 1 :]

    sent = []

    def send_piece(owner, q, target):
        copy = pltpu.make_async_remote_copy(
            src_ref=pack.at[owner, q],
            dst_ref=pack.at[owner, q],
            send_sem=p_send.at[len(sent)],
            recv_sem=p_recv.at[owner, q],
            device_id={"rows": target},
            device_id_type=MESH,
        )
        copy.start()
        sent.append(copy)

    def wait_piece(owner, q):
        pltpu.make_async_remote_copy(
            src_ref=pack.at[owner, q],
            dst_ref=pack.at[owner, q],
            send_sem=p_send.at[0],
            recv_sem=p_recv.at[owner, q],
            device_id={"rows": flip(me, 1)},
            device_id_type=MESH,
        ).wait_recv()

    step = learn_rate * 0.2 * math.sqrt(max(n * shard_rows, cols))

    def weight_of(i):
        for at, (r, c) in enumerate(places):
            tile = pack[i, at // half, at % half]
            full_v[cut(r), cut(c)] = tile
            if r != c:
                full_v[cut(c), cut(r)] = tile.T
        decay = 1.0 - learn_rate * weight_decay
        nw_ref[i] = (
            w_v[i].astype(F32) * decay - step * dot(send_v[i], full_v[...])
        ).astype(BF16)

    for level in range(bits):
        for q in range(2):
            send_piece(me, q, flip(me, 2 << orders[q][level]))
    for q in range(2):
        send_piece(me, q, flip(me, 1))
    load_w.wait()
    weight_of(me)
    masks = [[m for m in range(n // 2) if bin(m).count("1") == level] for level in range(bits + 1)]
    for level in range(bits + 1):
        if level > 0:
            pieces = [(m, q) for m in masks[level] for q in range(2)]
            for m, q in sorted(pieces, key=lambda at: -len(onward(*at))):
                wait_piece(owner_of(m), q)
                for b in onward(m, q):
                    send_piece(owner_of(m), q, flip(me, 2 << b))
                send_piece(owner_of(m), q, flip(me, 1))
            for m in masks[level]:
                weight_of(owner_of(m))
        for m in masks[level]:
            owner = flip(owner_of(m), 1)
            for q in range(2):
                wait_piece(owner, q)
            weight_of(owner)

    def drain_forward(k, carry):
        forward_copy(peer(k), me).wait_send()
        return carry

    lax.fori_loop(1, n, drain_forward, 0)
    lax.fori_loop(1, devices, drain_sum, 0)
    for copy in sent:
        copy.wait_send()


def local(weight, momentum, gradient, assign):
    n = lax.axis_size("rows")
    groups = lax.axis_size("experts")
    _, slots, shard_rows, cols = gradient.shape
    assert slots == n and n & (n - 1) == 0
    block_rows = min(1024, n * shard_rows)
    shape = (slots, shard_rows, cols)
    new_weight, new_momentum = pl.pallas_call(
        functools.partial(kernel, n, groups, block_rows),
        out_shape=(jax.ShapeDtypeStruct(shape, BF16),) * 2,
        in_specs=[pl.BlockSpec(memory_space=pltpu.HBM)] * 4,
        out_specs=(pl.BlockSpec(memory_space=pltpu.VMEM),) * 2,
        scratch_shapes=[pltpu.VMEM(shape, BF16)] * 5
        + [
            pltpu.VMEM((cols, cols), F32),
            pltpu.VMEM((cols, cols), BF16),
            pltpu.VMEM((cols, cols), BF16),
            pltpu.VMEM((n * groups, 8, 128), F32),
            pltpu.VMEM((n, 2, tiles * (tiles + 1) // 4, cols // tiles, cols // tiles), BF16),
            pltpu.VMEM((cols, cols), BF16),
            pltpu.SMEM((1, slots), jnp.int32),
            pltpu.SemaphoreType.DMA((3,)),
            pltpu.SemaphoreType.DMA((n,)),
            pltpu.SemaphoreType.DMA((n * groups,)),
            pltpu.SemaphoreType.DMA((n * groups,)),
            pltpu.SemaphoreType.DMA((n,)),
            pltpu.SemaphoreType.DMA((n,)),
            pltpu.SemaphoreType.DMA((2 * n,)),
            pltpu.SemaphoreType.DMA((n, 2)),
        ],
        compiler_params=pltpu.CompilerParams(
            collective_id=0, has_side_effects=True, vmem_limit_bytes=48 << 20
        ),
        name="muon_step",
    )(assign, weight[0], momentum[0], gradient[0])
    return new_weight[None], new_momentum[None]


def solution(mesh):
    placed = P("experts", None, "rows", None)
    return jax.shard_map(
        local,
        mesh=mesh,
        in_specs=(placed, placed, placed, P("experts", None)),
        out_specs=(placed, placed),
        check_vma=False,
    )
```
